32 devices in a mesh: groups: 2 (over x), exp: 16 (over z, y, core).
Axes of the slice: x: 2, y: 2, z: 4, core: 2. Of those that a mesh axis runs over, the one named last changes fastest.
Arguments:
- estimate: float32 [512, 4, 512], P('exp', 'groups'), parts along dimension 1, may hold values from -6 to 6
- observed: bfloat16 [32, 512, 512], P(('groups', 'exp')), parts along dimension 0, may hold values from -12 to 12
- pixel_mask: int32 [32, 512, 512], P(('groups', 'exp')), parts along dimension 0, may hold values 0 or 1
- blur_mix: float32 [32, 6, 8, 8], P(('groups', 'exp')), parts along dimension 0, may hold values from 0.2 to 1
- dithers: int32 [32, 2], P(('groups', 'exp')), parts along dimension 0, may hold values from -8 to 8, as said below
- patch_of: int32 [32], P(('groups', 'exp')), parts along dimension 0, may hold values from 0 to 1
- column_taps: bfloat16 [6, 15], replicated, may hold values from 0 to 0.119628906
- row_taps: bfloat16 [6, 15], replicated, may hold values from 0 to 0.119628906
Outputs:
- gradient: float32 [512, 4, 512], P('exp', 'groups'), parts along dimension 1
The draws below stay inside these ranges and needn't reach their ends.
There are 2 independent parts, one for each index of `groups`. The reference program is written for one: setup_inputs(seed, part) draws one part's arguments, and reference() takes and returns one part's arrays. A program takes and returns all parts, laid end to end along the dimension named above; an argument that names none is the same for every part. Nothing has to cross between parts.
Inputs may be any that keep to these rules, and one draw needn't show every extreme that they name: `dithers`: each exposure's two offsets; the value 8 occurs among the row offsets and -8 among the column offsets.
All inputs are finite; a program needn't handle non-finite values. No bound on the sum of `pixel_mask` on one device may be relied on, other than what follows from the above.
Results may differ from the reference program's by a relative error of at most 0.004.
Values may be sent and summed in bfloat16 or wider, within the bound.
No kernel may reach another device: no remote copies, remote signals or barrier semaphores. Data moves between devices by JAX's collectives and lax.ppermute only.
A program may use at most 128 MiB of HBM per device.

```python
import jax
import jax.numpy as jnp
from jax import lax

PATCH = 512
PATCHES = 2
BASES = 6
TAPS = 15
DMAX = 8
TILES = 8
EXPOSURES = 16


def draw_dithers(key, part):
    base_value = jax.random.randint(jax.random.fold_in(key, 11), (EXPOSURES, 2), -DMAX, DMAX + 1)
    chosen = jax.random.randint(jax.random.fold_in(key, 12), (2,), 0, EXPOSURES)
    row_ids = lax.broadcasted_iota(jnp.int32, (EXPOSURES, 2), 0)
    col_ids = lax.broadcasted_iota(jnp.int32, (EXPOSURES, 2), 1)
    base_value = jnp.where((row_ids == chosen[0]) & (col_ids == 0), DMAX, base_value)
    base_value = jnp.where((row_ids == chosen[1]) & (col_ids == 1), -DMAX, base_value)
    return base_value.astype(jnp.int32)


def set_ends(values, key, smallest, high):
    longest = values.shape.index(max(values.shape))
    spots = []
    for shift in (0, 1):
        where = [jax.random.randint(jax.random.fold_in(key, axis), (), 0, length) for axis, length in enumerate(values.shape)]
        where[longest] = (where[longest] + shift) % values.shape[longest]
        spots.append(tuple(where))
    return values.at[spots[0]].set(smallest).at[spots[1]].set(high)


def shard_levels(stream_key, shape, split, low, top_value):
    factor_of = 1.0
    for axis_at, parts in split:
        steps = jax.random.uniform(jax.random.fold_in(jax.random.fold_in(stream_key, 6), axis_at), (parts,), jnp.float32, low / len(split), top_value / len(split))
        factor_of = factor_of * jnp.repeat(jnp.exp(steps), shape[axis_at] // parts).reshape((-1,) + (1,) * (len(shape) - 1 - axis_at))
    return factor_of


def noise(rng, shape, spread, most, split=(), dtype=jnp.bfloat16):
    values = jax.random.normal(rng, shape, jnp.float32) * spread
    if len(split) > 0:
        values = shard_levels(rng, shape, split, -0.22, 0.18) * values
    return jnp.clip(values, min=-most, max=most).astype(dtype)


def setup_inputs(seed: int = 0, part: int = 0) -> dict:
    arg_keys = jax.random.split(jax.random.key(seed), 9)
    part_keys = jax.random.split(jax.random.fold_in(arg_keys[8], part), 9)
    return {
        "estimate": noise(part_keys[0], (PATCH, PATCHES, PATCH), 1.0, 6.0, ((0, 16),), jnp.float32),
        "observed": noise(part_keys[1], (EXPOSURES, PATCH, PATCH), 2.0, 12.0, ((0, 16),)),
        "pixel_mask": set_ends((jax.random.randint(part_keys[2], (EXPOSURES, PATCH, PATCH), 0, 10) < 9).astype(jnp.int32), jax.random.fold_in(part_keys[2], 1), 0, 1),
        "blur_mix": jnp.clip(0.2 + 0.8 * jax.random.uniform(part_keys[3], (EXPOSURES, BASES, TILES, TILES), jnp.float32) ** shard_levels(part_keys[3], (EXPOSURES, BASES, TILES, TILES), ((0, 16),), -0.2, 0.2), 0.2, 1.0),
        "dithers": draw_dithers(jax.random.fold_in(jax.random.fold_in(arg_keys[8], part), 71), part),
        "patch_of": set_ends(jax.random.randint(part_keys[5], (EXPOSURES,), 0, PATCHES), jax.random.fold_in(part_keys[5], 1), 0, PATCHES - 1).astype(jnp.int32),
        "column_taps": jnp.clip(jax.random.uniform(arg_keys[6], (BASES, TAPS), jnp.float32, 0.0, 0.119628906), 0.0, 0.119628906).astype(jnp.bfloat16),
        "row_taps": jnp.clip(jax.random.uniform(arg_keys[7], (BASES, TAPS), jnp.float32, 0.0, 0.119628906), 0.0, 0.119628906).astype(jnp.bfloat16),
    }


def band_stack(tap_values, extent, col_offset):
    half_width = tap_values.shape[1] // 2
    source = lax.broadcasted_iota(jnp.int32, (extent, extent), 0)
    target = lax.broadcasted_iota(jnp.int32, (extent, extent), 1)
    offset = source - target - col_offset + half_width
    inside = (source - col_offset >= 0) & (source - col_offset < extent)
    running = jnp.zeros((tap_values.shape[0], extent, extent), jnp.float32)
    for tap_index in range(tap_values.shape[1]):
        matches = ((offset == tap_index) & inside).astype(jnp.float32)
        running = running + tap_values[:, tap_index].astype(jnp.float32)[:, None, None] * matches[None]
    return running.astype(jnp.bfloat16)


def exposure_back(rowed, frame_data, mask_frame, blur_weights, row_shift, column_band):
    extent = frame_data.shape[0]
    basis_count = blur_weights.shape[0]
    tile_count = blur_weights.shape[1]
    tile_side = extent // tile_count
    padded = jnp.pad(rowed, ((DMAX, DMAX), (0, 0)))
    shifted = lax.dynamic_slice_in_dim(padded, DMAX + row_shift, extent, 0).reshape(extent, basis_count, extent)
    blurred = jnp.einsum("kba,bkc->kac", column_band.astype(jnp.float32), shifted.astype(jnp.float32))
    mix_full = jnp.broadcast_to(blur_weights[:, :, None, :, None], (basis_count, tile_count, tile_side, tile_count, tile_side)).reshape(basis_count, extent, extent)
    model_image = jnp.sum(mix_full * blurred, axis=0)
    residual = mask_frame.astype(jnp.float32) * (model_image - frame_data.astype(jnp.float32))
    weighted = (mix_full * residual[None]).astype(jnp.bfloat16)
    backed = jnp.einsum("kab,kbc->akc", column_band.astype(jnp.float32), weighted.astype(jnp.float32))
    backed = backed.astype(jnp.bfloat16).reshape(extent, basis_count * extent)
    return jnp.pad(backed, ((DMAX, DMAX), (0, 0)))


def back_rows(padded_back, back_stack, row_shift, patch_index, patch_count, first_row, row_count):
    picked = lax.dynamic_slice_in_dim(padded_back, first_row + DMAX - row_shift, row_count, 0)
    result = jnp.dot(picked, back_stack, preferred_element_type=jnp.float32)
    selector = lax.broadcasted_iota(jnp.int32, (1, patch_count, 1), 1) == patch_index
    return jnp.where(selector, result[:, None, :], jnp.zeros((), jnp.float32))


def reference(estimate, observed, pixel_mask, blur_mix, dithers, patch_of, column_taps, row_taps):
    extent = estimate.shape[0]
    patch_count = estimate.shape[1]
    estimate_low = estimate.astype(jnp.bfloat16)
    column_band = band_stack(column_taps, extent, 0)

    def one_exposure(running, packed):
        frame_data, mask_frame, blur_weights, shifts, patch_index = packed
        row_band = band_stack(row_taps, extent, shifts[1])
        forward_stack = jnp.transpose(row_band, (1, 0, 2)).reshape(extent, -1)
        back_stack = jnp.transpose(row_band, (0, 2, 1)).reshape(-1, extent)
        chosen = lax.dynamic_index_in_dim(estimate_low, patch_index, 1, keepdims=False)
        rowed = jnp.dot(chosen, forward_stack, preferred_element_type=jnp.float32).astype(jnp.bfloat16)
        padded_back = exposure_back(rowed, frame_data, mask_frame, blur_weights, shifts[0], column_band)
        term = back_rows(padded_back, back_stack, shifts[0], patch_index, patch_count, 0, extent)
        return running + term, None

    start_value = jnp.zeros((extent, patch_count, extent), jnp.float32)
    gradient, unused = lax.scan(one_exposure, start_value, (observed, pixel_mask, blur_mix, dithers, patch_of))
    return gradient
```

```python
import functools

import jax
import jax.numpy as jnp
from jax import lax
from jax.experimental import pallas as pl
from jax.experimental.pallas import tpu as pltpu
from jax.sharding import PartitionSpec as P

DMAX = 8
HALO = 16
LANES = 128
WINDOW = 256
PARTS = 3


VMEM = pl.BlockSpec(memory_space=pltpu.VMEM)
SMEM = pl.BlockSpec(memory_space=pltpu.SMEM)


def iota(shape, axis):
    return lax.broadcasted_iota(jnp.int32, shape, axis)


def toeplitz(taps_ref, basis, distance):
    total = jnp.zeros(distance.shape, jnp.float32)
    for tap in range(taps_ref.shape[1]):
        total = jnp.where(distance == tap, taps_ref[basis, tap], total)
    return total.astype(jnp.bfloat16)


def bands_kernel(half, tile_side, row_taps, column_taps, forward, backward, down, up, spread):
    bases = row_taps.shape[0]
    pad = (WINDOW - LANES) // 2
    far = iota((WINDOW, LANES), 0) - iota((WINDOW, LANES), 1)
    for k in range(bases):
        forward[:, k * LANES : (k + 1) * LANES] = toeplitz(row_taps, k, far - pad + half)
        backward[k * WINDOW : (k + 1) * WINDOW, :] = toeplitz(row_taps, k, pad + half - far)
        shape = down.shape[1:]
        down[k] = toeplitz(column_taps, k, iota(shape, 1) - iota(shape, 0) - (HALO - 2 * half))
        shape = up.shape[1:]
        up[k] = toeplitz(column_taps, k, iota(shape, 0) - iota(shape, 1) + 2 * half)
    owner = iota(spread.shape, 1) // tile_side
    spread[...] = (owner == iota(spread.shape, 0)).astype(jnp.bfloat16)


def pack_kernel(chunk, half, dithers, patch, observed, mask, mix, out, seen, good):
    extent = observed.shape[0]
    groups, rows = out.shape[0], out.shape[1]
    window = (rows - 8) // 2
    shift = dithers[0, 0]
    for ref, source in ((seen, observed), (good, mask)):
        ref[0:HALO, :] = jnp.zeros((HALO, extent), jnp.float32)
        ref[HALO : HALO + extent, :] = source[...].astype(jnp.float32)
        tail = ref.shape[0] - HALO - extent
        ref[HALO + extent :, :] = jnp.zeros((tail, extent), jnp.float32)
        ref[...] = pltpu.roll(ref[...], ref.shape[0] - HALO + shift + half, 0)
    weights = mix[...]
    high = weights.astype(jnp.bfloat16)
    rest = weights - high.astype(jnp.float32)
    middle = rest.astype(jnp.bfloat16)
    low = (rest - middle.astype(jnp.float32)).astype(jnp.bfloat16)
    lane = iota((8, LANES), 1)
    facts = jnp.where(lane == 0, shift, jnp.where(lane == 1, dithers[0, 1], patch[0]))
    facts = facts.astype(jnp.float32).astype(jnp.bfloat16)
    for c in range(groups):
        out[c, 0:window, :] = seen[chunk * c : chunk * c + window, :].astype(jnp.bfloat16)
        out[c, window : 2 * window, :] = good[chunk * c : chunk * c + window, :].astype(jnp.bfloat16)
        for at, part in enumerate((high, middle, low, facts)):
            out[c, 2 * window :, at * LANES : (at + 1) * LANES] = part


def join_kernel(count, group_size, *refs):
    pieces, (chunk, top, bottom) = refs[:-3], refs[-3:]
    group = lax.axis_index("exp") // group_size
    rows = pieces[0].shape[1]
    for m, piece in enumerate(pieces):
        if len(pieces) == 1:
            chunk[...] = piece[...]
        else:
            block = lax.rem(group - m + count, count)
            chunk[:, pl.ds(pl.multiple_of(block * rows, rows), rows), :] = piece[...]
    top[...] = chunk[:, 0:HALO, :]
    bottom[...] = chunk[:, chunk.shape[1] - HALO :, :]


def main_kernel(
    group_size, count, half, tiles,
    above, chunk, below, forward, backward, down, up, spread, *refs
):
    messages, outs, scratch = refs[:group_size], refs[group_size:-6], refs[-6:]
    patches, rowed, mixed, columns, backed, total = scratch
    bases, window, tall = down.shape
    rows = up.shape[1]
    extent = chunk.shape[2]
    wide = extent + LANES
    pad = (WINDOW - LANES) // 2
    tile_side = extent // tiles
    index = lax.axis_index("exp")
    place = lax.rem(index, group_size)
    group = index // group_size
    first = place * rows
    patches[:, 0:HALO, 0:extent] = above[...].astype(jnp.float32)
    patches[:, HALO : HALO + rows, 0:extent] = chunk[...].astype(jnp.float32)
    patches[:, HALO + rows :, 0:extent] = below[...].astype(jnp.float32)
    patches[:, :, extent:] = jnp.zeros(patches.shape[:2] + (LANES,), jnp.float32)
    total[...] = jnp.zeros(total.shape, jnp.float32)

    for message in messages:
        facts = message[2 * window :, PARTS * LANES :].astype(jnp.float32)
        lane = iota(facts.shape, 1)
        row_shift = jnp.max(jnp.where(lane == 0, facts, -100.0)).astype(jnp.int32)
        column_shift = jnp.max(jnp.where(lane == 1, facts, -100.0)).astype(jnp.int32)
        patch = jnp.max(jnp.where(lane == 2, facts, -100.0)).astype(jnp.int32)

        rolled = pltpu.roll(patches[patch], pad - column_shift, 1)
        row = iota((tall, wide), 0) + (first - HALO)
        column = iota((tall, wide), 1)
        keep = (row >= jnp.maximum(row_shift, 0)) & (row < extent + jnp.minimum(row_shift, 0))
        keep = keep & (column >= pad) & (column < extent + pad)
        moved = jnp.where(keep, rolled, 0.0).astype(jnp.bfloat16)
        for c in range(extent // LANES):
            piece = jnp.dot(
                moved[:, c * LANES : c * LANES + WINDOW], forward[...],
                preferred_element_type=jnp.float32,
            ).astype(jnp.bfloat16)
            for k in range(bases):
                at = k * extent + c * LANES
                rowed[:, at : at + LANES] = piece[:, k * LANES : (k + 1) * LANES]

        for part in range(PARTS):
            compact = message[2 * window :, part * LANES : (part + 1) * LANES]
            columns[part * 8 : (part + 1) * 8, :] = jnp.dot(
                compact, spread[...], preferred_element_type=jnp.float32
            ).astype(jnp.bfloat16)
        low = (lax.rem(iota((window, PARTS * 8), 1), 8)) * tile_side
        at = iota((window, PARTS * 8), 0) + (first - row_shift - half)
        pick = ((at >= low) & (at < low + tile_side)).astype(jnp.float32).astype(jnp.bfloat16)

        model = jnp.zeros((window, extent), jnp.float32)
        for k in range(bases):
            span = slice(k * extent, (k + 1) * extent)
            blurred = jnp.dot(down[k], rowed[:, span], preferred_element_type=jnp.float32)
            weight = jnp.dot(pick, columns[:, span], preferred_element_type=jnp.float32)
            mixed[k] = weight
            model = model + weight * blurred
        seen = message[0:window, :].astype(jnp.float32)
        good = message[window : 2 * window, :].astype(jnp.float32)
        residual = good * (model - seen)
        for k in range(bases):
            weighted = (mixed[k] * residual).astype(jnp.bfloat16)
            backed[k] = jnp.dot(
                up[k], weighted, preferred_element_type=jnp.float32
            ).astype(jnp.bfloat16)

        strips = []
        for c in range(-1, extent // LANES):
            low_at, high_at = max(c * LANES, 0), min(c * LANES + WINDOW, extent)
            skip = low_at - c * LANES
            size = high_at - low_at
            left = jnp.concatenate([backed[k, :, low_at:high_at] for k in range(bases)], axis=1)
            right = jnp.concatenate(
                [backward[k * WINDOW + skip : k * WINDOW + skip + size, :] for k in range(bases)],
                axis=0,
            )
            strips.append(jnp.dot(left, right, preferred_element_type=jnp.float32))
        term = jnp.concatenate(strips, axis=1)
        row = iota((rows, wide), 0) + first
        column = iota((rows, wide), 1)
        keep = (row >= row_shift) & (row < extent + row_shift)
        keep = keep & (column >= pad) & (column < extent + pad)
        term = pltpu.roll(jnp.where(keep, term, 0.0), wide - pad + column_shift, 1)
        total[patch] = total[patch] + term[:, 0:extent]

    block = outs[0].shape[1]
    if len(outs) == 1:
        outs[0][...] = total[...].astype(jnp.bfloat16)
        return
    for m in range(count):
        owner = lax.rem(group - m + count, count)
        span = pl.ds(pl.multiple_of(owner * block, block), block)
        outs[m][...] = total[:, span, :].astype(jnp.bfloat16)


def sum_kernel(count, *refs):
    pieces, out = refs[:count], refs[count]
    for q in range(pieces[0].shape[0]):
        running = pieces[0][q].astype(jnp.float32)
        for piece in pieces[1:]:
            running = running + piece[q].astype(jnp.float32)
        out[:, q, :] = running


def call(kernel, out_shape, operands, smem=(), scratch=(), name=None):
    specs = [SMEM if at in smem else VMEM for at in range(len(operands))]
    outs = jax.tree.map(lambda _: VMEM, out_shape)
    return pl.pallas_call(
        kernel,
        out_shape=out_shape,
        in_specs=specs,
        out_specs=outs,
        scratch_shapes=list(scratch),
        compiler_params=pltpu.CompilerParams(vmem_limit_bytes=48 << 20),
        name=name,
    )(*operands)


def per_device(devices, group_size, estimate, observed, pixel_mask, blur_mix, dithers, patch_of, column_taps, row_taps):
    extent = observed.shape[1]
    patch_count = estimate.shape[1]
    block = estimate.shape[0]
    bases, tap_count = row_taps.shape
    tiles = blur_mix.shape[2]
    half = tap_count // 2
    count = devices // group_size
    rows = extent // group_size
    window = rows + HALO
    tall = rows + 2 * HALO
    low, wide = jnp.bfloat16, jnp.float32
    shape = jax.ShapeDtypeStruct

    mix = jnp.pad(jnp.transpose(blur_mix[0], (1, 0, 2)).reshape(tiles, bases * tiles), ((0, 8 - tiles), (0, LANES - bases * tiles)))
    message = call(
        functools.partial(pack_kernel, rows, half),
        shape((group_size, 2 * window + 8, extent), low),
        (dithers, patch_of, observed[0], pixel_mask[0], mix),
        smem=(0, 1),
        scratch=[pltpu.VMEM((extent + 4 * HALO, extent), wide)] * 2,
        name="pack",
    )
    index = lax.axis_index("exp")
    place = lax.rem(index, group_size)

    own = jnp.transpose(estimate.astype(low), (1, 0, 2))
    pieces = []
    for m in range(count):
        pairs = [(b, (b + m) % count * group_size + b // count) for b in range(devices)]
        pieces.append(lax.ppermute(own, "exp", pairs))
    messages = [lax.dynamic_index_in_dim(message, place, 0, keepdims=False)]
    for step in range(1, group_size):
        send = lax.dynamic_index_in_dim(message, place ^ step, 0, keepdims=False)
        pairs = [(d, d ^ step) for d in range(devices)]
        messages.append(lax.ppermute(send, "exp", pairs))
    whole_tiles = block % 16 == 0 and count > 1
    order = lax.rem(index // group_size - jnp.arange(count) + count, count)
    if not whole_tiles:
        stacked = jnp.take(jnp.stack(pieces, 1), order, axis=1)
        pieces = [stacked.reshape(patch_count, rows, extent)]
    chunk, top, bottom = call(
        functools.partial(join_kernel, count, group_size),
        (
            shape((patch_count, rows, extent), low),
            shape((patch_count, HALO, extent), low),
            shape((patch_count, HALO, extent), low),
        ),
        pieces,
        name="join",
    )
    line = [d for d in range(devices) if d % group_size < group_size - 1]
    above = lax.ppermute(bottom, "exp", [(d, d + 1) for d in line])
    below = lax.ppermute(top, "exp", [(d + 1, d) for d in line])
    bands = call(
        functools.partial(bands_kernel, half, extent // tiles),
        (
            shape((WINDOW, bases * LANES), low),
            shape((bases * WINDOW, LANES), low),
            shape((bases, window, tall), low),
            shape((bases, rows, window), low),
            shape((LANES, bases * extent), low),
        ),
        (row_taps.astype(wide), column_taps.astype(wide)),
        smem=(0, 1),
        name="bands",
    )
    sums = call(
        functools.partial(main_kernel, group_size, count, half, tiles),
        [shape((patch_count, block if whole_tiles else rows, extent), low)] * (count if whole_tiles else 1),
        (above, chunk, below, *bands, *messages),
        scratch=[
            pltpu.VMEM((patch_count, tall, extent + LANES), wide),
            pltpu.VMEM((tall, bases * extent), low),
            pltpu.VMEM((bases, window, extent), wide),
            pltpu.VMEM((PARTS * 8, bases * extent), low),
            pltpu.VMEM((bases, rows, extent), low),
            pltpu.VMEM((patch_count, rows, extent), wide),
        ],
        name="main",
    )
    if not whole_tiles:
        stacked = sums[0].reshape(patch_count, count, block, extent)
        sums = list(jnp.take(stacked, order, axis=1).transpose(1, 0, 2, 3))
    parts = []
    for m in range(count):
        pairs = [((b + m) % count * group_size + b // count, b) for b in range(devices)]
        parts.append(lax.ppermute(sums[m], "exp", pairs))
    return call(
        functools.partial(sum_kernel, count),
        shape(estimate.shape, wide),
        parts,
        name="finish",
    )


def solution(mesh):
    devices = mesh.shape["exp"]
    group_size = 2 ** ((devices.bit_length() - 1) // 2)
    in_specs = (
        P("exp", "groups", None),
        P(("groups", "exp"), None, None),
        P(("groups", "exp"), None, None),
        P(("groups", "exp"), None, None, None),
        P(("groups", "exp"), None),
        P(("groups", "exp")),
        P(),
        P(),
    )
    return jax.shard_map(
        functools.partial(per_device, devices, group_size),
        mesh=mesh, in_specs=in_specs, out_specs=P("exp", "groups", None), check_vma=False,
    )
```
